32 devices in a mesh: cl: 8 (over z, x), hot: 4 (over y, core).
Axes of the slice: x: 2, y: 2, z: 4, core: 2. Of those that a mesh axis runs over, the one named last changes fastest.
Arguments:
- documents: bfloat16 [4096, 768], P(('cl', 'hot')), may hold values from -6 to 6
- cold_weight: bfloat16 [16, 128, 768], P('cl'), may hold values from -0.21875 to 0.21875
- hot_weight: bfloat16 [1024, 768], P('hot'), may hold values from -0.21875 to 0.21875
- shortlist: int32 [4096, 4], P(('cl', 'hot')), may hold values from 0 to 15, all different within a row; in each aligned block of 128 rows (0 to 127, 128 to 255, ...) at most 64 rows name the same one
- positives: int32 [4096, 4], P(('cl', 'hot')), may hold values from 0 to 128
- hot_ids: int32 [4096, 2], P(('cl', 'hot')), may hold values from 0 to 7, all different within a row
- hot_labels: int32 [4096, 2], P(('cl', 'hot')), may hold values from 0 to 128
Outputs:
- grad_cold: float32 [16, 128, 768], P('cl')
- grad_hot: float32 [1024, 768], P('hot')
- grad_docs: bfloat16 [4096, 768], P(('cl', 'hot'))
The draws below stay inside these ranges and needn't reach their ends.
Inputs may be any that keep to these rules, and one draw needn't show every extreme that they name: `shortlist`: each row names 4 different clusters. Among the 128 rows of one device no cluster is named more than 64 times, a bound that some block reaches. `positives`: the value 128 means that the cluster holds no positive label of the document. `hot_ids`: each row names 2 different hot clusters. `hot_labels`: the value 128 means that the hot cluster holds no positive label of the document.
All inputs are finite; a program needn't handle non-finite values.
Results may differ from the reference program's by a relative error of at most 0.0085.
Values may be sent and summed in bfloat16 or wider, within the bound.
No kernel may reach another device: no remote copies, remote signals or barrier semaphores. Data moves between devices by JAX's collectives and lax.ppermute only.
A program may use at most 64 MiB of HBM per device.

```python
import math
import jax
import jax.numpy as jnp
import numpy as np
from jax import lax

D = 768
LB = 128
S = 4
HS = 2
DOC_DEV = 128
CLUSTERS = 16
HOT = 8
DOCS = 4096
CAPC = 64
N_CL = 8
N_HOT = 4


def touch_ends(array, own_key, least, top_value):
    index_at = [jax.random.randint(jax.random.fold_in(own_key, axis), (), 0, length) for axis, length in enumerate(array.shape)]
    main_axis = array.shape.index(max(array.shape))
    neighbour = index_at[:main_axis] + [(index_at[main_axis] + 1) % array.shape[main_axis]] + index_at[main_axis + 1:]
    return array.at[tuple(index_at)].set(least).at[tuple(neighbour)].set(top_value)


def block_scale(key, extent, pieces, low, top_value):
    factor_of = 1.0
    for axis_at, blocks in pieces:
        steps = jax.random.uniform(jax.random.fold_in(jax.random.fold_in(key, 6), axis_at), (blocks,), jnp.float32, low / len(pieces), top_value / len(pieces))
        factor_of = factor_of * jnp.repeat(jnp.exp(steps), extent[axis_at] // blocks).reshape((-1,) + (1,) * (len(extent) - 1 - axis_at))
    return factor_of


def choose_distinct(rng, rows, count, top, lift):
    order = jax.random.permutation(jax.random.fold_in(rng, 1), count)
    boost = order
    for power in range(3):
        boost = boost * boost // count
    boost = boost * lift // count
    lots = jax.random.randint(jax.random.fold_in(rng, 2), (rows, count), 0, 4096) + boost
    holders = jax.random.permutation(jax.random.fold_in(rng, 3), rows)[jnp.arange(count) % rows]
    lots = jnp.where(jnp.arange(rows)[:, None] == holders[None, :], 1 << 14, lots)
    score = lots * count + jnp.arange(count)
    return lax.top_k(score.astype(jnp.int32), top)[1].astype(jnp.int32)


def assign_block(stream_key, own, number, rows, amount, top, most, slope):
    order = jax.random.permutation(stream_key, amount)
    packed, usual = portions_of(amount, rows * top, most, slope, True), portions_of(amount, rows * top, most, slope, False)
    places = jnp.arange(amount)

    def named(sizes, rotation):
        used = int((sizes > 0).sum())
        fixed = max(1, used // 4)
        shifted = fixed + (places - fixed + rotation * (used - fixed)) % max(1, amount - fixed)
        return jnp.zeros((amount,), jnp.int32).at[order[jnp.where(places < fixed, places, shifted)]].set(jnp.asarray(sizes, jnp.int32))

    sizes = jnp.where(number % 4 == 0, named(packed, number // 4), named(usual, number - number // 4 - 1))
    mixed = jax.random.permutation(jax.random.fold_in(own, 3), amount)
    source_of, receiver = mixed[0:amount // 2 * 2:2], mixed[1:amount // 2 * 2:2]
    margin = jnp.minimum(sizes[source_of] - 1, most - sizes[receiver]) // 2
    margin = jnp.where((source_of == order[0]) | (receiver == order[0]) | (sizes[receiver] == 0), 0, jnp.maximum(margin, 0))
    shifted = jax.random.randint(jax.random.fold_in(own, 4), (amount // 2,), 0, 1 << 20) % (margin + 1)
    sizes = sizes.at[source_of].add(-shifted).at[receiver].add(shifted)
    items = jnp.searchsorted(jnp.cumsum(sizes), jnp.arange(rows * top), side="right").astype(jnp.int32)
    grid = items.reshape(top, rows).T
    grid = grid[jax.random.permutation(jax.random.fold_in(own, 1), rows)]
    rotation = jax.random.randint(jax.random.fold_in(own, 2), (rows, 1), 0, top)
    return jnp.take_along_axis(grid, (jnp.arange(top)[None, :] + rotation) % top, axis=1)


def portions_of(amount, total, limit, lean, full):
    loads = [(1 << 20) // math.isqrt(standing ** lean) + 1 for standing in range(1, amount + 1)]
    largest = limit if full else min(limit, max(-(-total // amount), total * loads[0] // sum(loads)))
    least = 1 if total - largest >= amount - 1 else 0
    counts, spare = [largest] + [least] * (amount - 1), total - largest - least * (amount - 1)
    while spare > 0:
        movable = [i for i in range(1, amount) if counts[i] < largest] or [i for i in range(1, amount) if counts[i] < limit]
        mass, budget = sum([loads[i] for i in movable]), spare
        for i in movable:
            extra = min(limit - counts[i], max(1, budget * loads[i] // mass), spare)
            counts[i] = counts[i] + extra
            spare = spare - extra
    return np.array(counts)


def centred(stream_key, shape, width, most, cuts=(), held_as=jnp.bfloat16):
    array = jax.random.normal(stream_key, shape, jnp.float32) * width
    if len(cuts) > 0:
        array = block_scale(stream_key, shape, cuts, -0.22, 0.18) * array
    return jnp.clip(array, min=-most, max=most).astype(held_as)


def setup_inputs(seed: int = 0) -> dict:
    seeds = jax.random.split(jax.random.key(seed), 8)
    documents = centred(seeds[0], (DOCS, D), 1.0, 6.0, ((0, 32),))
    cold_weight = centred(seeds[1], (CLUSTERS, LB, D), D ** -0.5, 0.21875, ((0, 8),))
    hot_weight = centred(seeds[2], (HOT * LB, D), D ** -0.5, 0.21875, ((0, 4),))
    shortlist_keys = jax.random.split(jax.random.fold_in(seeds[3], 1), DOCS // DOC_DEV)
    shortlist_turns = jax.random.permutation(jax.random.fold_in(seeds[3], 3), DOCS // DOC_DEV)
    shortlist = jax.vmap(lambda own, number: assign_block(jax.random.fold_in(seeds[3], 2), own, number, DOC_DEV, CLUSTERS, S, CAPC, 2))(shortlist_keys, shortlist_turns).reshape((DOCS, S))
    positives = touch_ends(jax.random.randint(seeds[4], (DOCS, S), 0, LB + 1), jax.random.fold_in(seeds[4], 1), 0, LB).astype(jnp.int32)
    hot_ids = choose_distinct(seeds[5], DOCS, HOT, HS, 4096)
    hot_labels = touch_ends(jax.random.randint(seeds[6], (DOCS, HS), 0, LB + 1), jax.random.fold_in(seeds[6], 1), 0, LB).astype(jnp.int32)
    return {"documents": documents, "cold_weight": cold_weight, "hot_weight": hot_weight, "shortlist": shortlist, "positives": positives, "hot_ids": hot_ids, "hot_labels": hot_labels}


def slot_index(short_rows, clusters, capacity):
    flat_ids = short_rows.reshape(-1)
    onehot = (flat_ids[:, None] == jnp.arange(clusters, dtype=jnp.int32)[None, :]).astype(jnp.int32)
    before = jnp.cumsum(onehot, axis=0, dtype=jnp.int32) - onehot
    return (flat_ids * capacity + lax.optimization_barrier(jnp.sum(before * onehot, axis=1))).astype(jnp.int32)

def hot_tag_table(hot_rows, label_rows, hot_count):
    matched = hot_rows[:, :, None] == jnp.arange(hot_count, dtype=jnp.int32)[None, None, :]
    return lax.optimization_barrier(jnp.sum(jnp.where(matched, label_rows[:, :, None] + 1, 0), axis=1)).astype(jnp.int32) - 1

def score_grad(scores, tag_values, label_ids):
    target = (tag_values == label_ids).astype(jnp.float32)
    live_mask = (tag_values >= 0).astype(jnp.float32)
    return ((jax.nn.sigmoid(scores) - target) * live_mask).astype(jnp.bfloat16)

def reference(documents, cold_weight, hot_weight, shortlist, positives, hot_ids, hot_labels):
    device_count = N_CL * N_HOT
    highest = lax.Precision.HIGHEST
    label_axis = jnp.arange(LB, dtype=jnp.float32)
    hot_columns = (jnp.arange(HOT * LB, dtype=jnp.int32) % LB).astype(jnp.float32)
    cold_full = cold_weight.astype(jnp.float32)
    hot_full = hot_weight.astype(jnp.float32)

    def one_device(carry, inputs):
        cold_accum, hot_accum = carry
        doc_rows, short_rows, pos_rows, hid_rows, hlab_rows = inputs
        slot_ids = slot_index(short_rows, CLUSTERS, CAPC)
        repeated = jnp.repeat(doc_rows, S, axis=0)
        outgoing = jnp.zeros((CLUSTERS * CAPC, D), jnp.bfloat16).at[slot_ids].set(repeated)
        tagged = jnp.full((CLUSTERS * CAPC,), -1.0, jnp.float32).at[slot_ids].set(pos_rows.reshape(-1).astype(jnp.float32))
        rows_full = outgoing.reshape(CLUSTERS, CAPC, D).astype(jnp.float32)
        scores = jnp.einsum('krd,kld->krl', rows_full, cold_full, precision=highest)
        pair_grads = score_grad(scores, tagged.reshape(CLUSTERS, CAPC)[..., None], label_axis)
        grads_full = pair_grads.astype(jnp.float32)
        cold_accum = cold_accum + jnp.einsum('krl,krd->kld', grads_full, rows_full, precision=highest)
        row_grads = jnp.einsum('krl,kld->krd', grads_full, cold_full, precision=highest).astype(jnp.bfloat16)
        picked = row_grads.reshape(CLUSTERS * CAPC, D)[slot_ids].astype(jnp.float32)
        cold_rows = lax.optimization_barrier(jnp.sum(picked.reshape(DOC_DEV, S, D), axis=1))
        tag_cols = jnp.repeat(hot_tag_table(hid_rows, hlab_rows, HOT).astype(jnp.float32), LB, axis=1)
        doc_full = doc_rows.astype(jnp.float32)
        scores_hot = jnp.dot(doc_full, hot_full.T, precision=highest)
        hot_grads = score_grad(scores_hot, tag_cols, hot_columns).astype(jnp.float32)
        hot_accum = hot_accum + jnp.dot(hot_grads.T, doc_full, precision=highest)
        hot_rows = jnp.dot(hot_grads, hot_full, precision=highest)
        return ((cold_accum, hot_accum), (cold_rows + hot_rows).astype(jnp.bfloat16))
    inputs = (documents.reshape(device_count, DOC_DEV, D), shortlist.reshape(device_count, DOC_DEV, S), positives.reshape(device_count, DOC_DEV, S), hot_ids.reshape(device_count, DOC_DEV, HS), hot_labels.reshape(device_count, DOC_DEV, HS))
    initial = (jnp.zeros((CLUSTERS, LB, D), jnp.float32), jnp.zeros((HOT * LB, D), jnp.float32))
    (grad_cold, grad_hot), doc_grads = lax.scan(one_device, initial, inputs)
    return (grad_cold, grad_hot, doc_grads.reshape(DOCS, D))
```

```python
import jax
import jax.numpy as jnp
from jax import lax
from jax.experimental import pallas as pl
from jax.experimental.pallas import tpu as pltpu
from jax.sharding import PartitionSpec as P

AXES = ("cl", "hot")
BF = jnp.bfloat16
F32 = jnp.float32


def slot_index(short_rows, clusters, capacity):
    flat_ids = short_rows.reshape(-1)
    onehot = (flat_ids[:, None] == jnp.arange(clusters, dtype=jnp.int32)[None, :]).astype(jnp.int32)
    before = jnp.cumsum(onehot, axis=0, dtype=jnp.int32) - onehot
    return flat_ids * capacity + jnp.sum(before * onehot, axis=1)


def hot_tag_table(hot_rows, label_rows, hot_count):
    matched = hot_rows[:, :, None] == jnp.arange(hot_count, dtype=jnp.int32)[None, None, :]
    return jnp.sum(jnp.where(matched, label_rows[:, :, None] + 1, 0), axis=1) - 1


def score_grad(scores, tag_values, label_ids):
    target = (tag_values == label_ids).astype(jnp.float32)
    live_mask = (tag_values >= 0).astype(jnp.float32)
    return ((jax.nn.sigmoid(scores) - target) * live_mask).astype(jnp.bfloat16)


def general_form(documents, cold_weight, hot_weight, shortlist, positives, hot_ids, hot_labels):
    doc_rows, feature_width = documents.shape
    short_count = shortlist.shape[1]
    local_clusters, label_count = (cold_weight.shape[0], cold_weight.shape[1])
    owners = lax.axis_size("cl")
    clusters = local_clusters * owners
    capacity = max(4, 2 * doc_rows * short_count // clusters)
    slot_ids = slot_index(shortlist, clusters, capacity)
    repeated = jnp.repeat(documents, short_count, axis=0)
    outgoing = (
        jnp.zeros((clusters * capacity, feature_width), jnp.bfloat16).at[slot_ids].set(repeated)
    )
    tagged = (
        jnp.full((clusters * capacity,), -1.0, jnp.float32)
        .at[slot_ids]
        .set(positives.reshape(-1).astype(jnp.float32))
    )
    outgoing = outgoing.reshape(owners, local_clusters, capacity, feature_width)
    tagged = tagged.astype(jnp.bfloat16).reshape(owners, local_clusters, capacity)
    arrived, arrived_tags = (
        lax.all_to_all(outgoing, "cl", split_axis=0, concat_axis=0, tiled=True),
        lax.all_to_all(tagged, "cl", split_axis=0, concat_axis=0, tiled=True),
    )
    scores = jnp.einsum("skrd,kld->skrl", arrived, cold_weight, preferred_element_type=jnp.float32)
    label_axis = jnp.arange(label_count, dtype=jnp.float32)
    pair_grads = score_grad(scores, arrived_tags.astype(jnp.float32)[..., None], label_axis)
    cold_term = jnp.einsum(
        "skrl,skrd->kld", pair_grads, arrived, preferred_element_type=jnp.float32
    )
    row_grads = jnp.einsum(
        "skrl,kld->skrd", pair_grads, cold_weight, preferred_element_type=jnp.float32
    ).astype(jnp.bfloat16)
    returned = lax.all_to_all(row_grads, "cl", split_axis=0, concat_axis=0, tiled=True)
    picked = returned.reshape(clusters * capacity, feature_width)[slot_ids].astype(jnp.float32)
    cold_rows = jnp.sum(picked.reshape(doc_rows, short_count, feature_width), axis=1)
    grad_cold = lax.psum(cold_term, "hot")
    replicas = lax.axis_size("hot")
    hot_local = hot_weight.shape[0] // label_count
    hot_count = hot_local * replicas
    tag_table = hot_tag_table(hot_ids, hot_labels, hot_count)
    tag_cols = jnp.repeat(tag_table.astype(jnp.float32), label_count, axis=1)
    weights_part = lax.all_gather(hot_weight, "hot", axis=0, tiled=True)
    length = weights_part.shape[0]
    scores_hot = lax.dot_general(
        documents, weights_part, (((1,), (1,)), ((), ())), preferred_element_type=jnp.float32
    )
    col_labels = (jnp.arange(length, dtype=jnp.int32) % label_count).astype(jnp.float32)
    piece_grads = score_grad(scores_hot, tag_cols, col_labels)
    accumulated = jnp.dot(piece_grads, weights_part, preferred_element_type=jnp.float32)
    hot_term = lax.psum_scatter(
        lax.dot_general(
            piece_grads, documents, (((0,), (0,)), ((), ())), preferred_element_type=jnp.float32
        ).astype(jnp.bfloat16),
        "hot",
        scatter_dimension=0,
        tiled=True,
    ).astype(jnp.float32)
    grad_hot = lax.psum(hot_term, "cl")
    grad_docs = (cold_rows + accumulated).astype(jnp.bfloat16)
    return (grad_cold, grad_hot, grad_docs)


ZN, XN, YN, KN = 4, 2, 2, 2
META = 16


def perm(move):
    pairs = []
    for z in range(ZN):
        for x in range(XN):
            for y in range(YN):
                for k in range(KN):
                    a, b, c, d = move(z, x, y, k)
                    src = ((z * XN + x) * YN + y) * KN + k
                    pairs.append((src, ((a * XN + b) * YN + c) * KN + d))
    return pairs


TO_X = perm(lambda z, x, y, k: (z, 1 - x, y, k))
TO_Y = perm(lambda z, x, y, k: (z, x, 1 - y, k))
TO_XY = perm(lambda z, x, y, k: (z, 1 - x, 1 - y, k))
TO_K = perm(lambda z, x, y, k: (z, x, y, 1 - k))
TO_Z = {s: perm(lambda z, x, y, k, s=s: ((z + s) % ZN, x, y, k)) for s in (1, 2, 3)}
PAIR_Z1 = perm(lambda z, x, y, k: (z ^ 1, x, y, k))
PAIR_Z2 = perm(lambda z, x, y, k: (z ^ 2, x, y, k))


def send(value, pairs):
    return lax.ppermute(value, AXES, pairs)


def position():
    cl = lax.axis_index("cl")
    hot = lax.axis_index("hot")
    return cl // XN, cl % XN, hot // KN, hot % KN


def dot(a, b, ca, cb):
    return lax.dot_general(a, b, (((ca,), (cb,)), ((), ())), preferred_element_type=F32)


def prep_kernel(docs, short, pos, hid, hlab, cold, msg, quarter):
    rows = docs.shape[0]
    _, _, y, k = position()
    half = quarter.shape[0]
    msg[0:rows, :] = docs[...]
    eye = (
        lax.broadcasted_iota(jnp.int32, (rows, rows), 0)
        == lax.broadcasted_iota(jnp.int32, (rows, rows), 1)
    ).astype(F32)
    fields = [dot(r[...].astype(F32), eye, 0, 0) for r in (short, pos, hid, hlab)]
    used = sum(f.shape[0] for f in fields)
    fields.append(jnp.zeros((META - used, rows), F32))
    msg[rows : rows + META, 0:rows] = jnp.concatenate(fields, axis=0).astype(BF)
    quarter[...] = cold[y, pl.ds(pl.multiple_of(k * half, half), half), :]


def prep(documents, shortlist, positives, hot_ids, hot_labels, cold_weight):
    rows, width = documents.shape
    half = cold_weight.shape[1] // KN
    return pl.pallas_call(
        prep_kernel,
        out_shape=(
            jax.ShapeDtypeStruct((rows + META, width), BF),
            jax.ShapeDtypeStruct((half, width), BF),
        ),
        name="prep",
    )(documents, shortlist, positives, hot_ids, hot_labels, cold_weight)


def pair_grad(scores, tag, first_label):
    labels = lax.broadcasted_iota(jnp.int32, scores.shape, 0).astype(F32) + first_label
    target = jnp.where(labels == tag, 1.0, 0.0)
    return jnp.where(tag >= 0.0, jax.nn.sigmoid(scores) - target, 0.0).astype(BF)


def scores_kernel(short_count, hot_count, *refs):
    msgs, refs = refs[:8], refs[8:]
    wq, (hot, mine, other, hotp, c0, c1, c2, c3) = refs[:4], refs[4:12]
    docs_s, meta_s, w_s, g_s, sems = refs[12:]
    rows = msgs[0].shape[0] - META
    quarter = wq[0].shape[0]
    labels = hotp.shape[0]
    z, x, y, k = position()
    copies = []

    def fetch(src, dst):
        c = pltpu.make_async_copy(src, dst, sems.at[len(copies)])
        c.start()
        copies.append(c)

    for i, m in enumerate(msgs):
        fetch(m.at[0:rows, :], docs_s.at[i * rows : (i + 1) * rows, :])
        fetch(m.at[rows : rows + META, 0:rows], meta_s.at[i])
    for s, w in enumerate(wq):
        fetch(w, w_s.at[s * quarter : (s + 1) * quarter, :])
    fetch(hot.at[pl.ds(pl.multiple_of(x * labels, labels), labels), :], w_s.at[4 * quarter :, :])
    for c in copies:
        c.wait()

    fields = [meta_s[i].astype(F32) for i in range(8)]
    meta = jnp.concatenate(fields, axis=1)

    def tag_of(cluster, at, count):
        tag = jnp.full((1, meta.shape[1]), -1.0, F32)
        for j in range(count):
            hit = meta[at + j : at + j + 1, :] == cluster
            tag = tag + jnp.where(hit, meta[at + count + j : at + count + j + 1, :] + 1.0, 0.0)
        return tag

    scores = dot(w_s[...], docs_s[...], 1, 1)
    first = (k * quarter).astype(F32)
    for s in range(4):
        owner = lax.rem(z + ZN - s, ZN) * XN + x
        tag = tag_of((owner * YN + y).astype(F32), 0, short_count)
        at = slice(s * quarter, (s + 1) * quarter)
        g_s[at, :] = pair_grad(scores[at, :], tag, first)
    tag = tag_of(((y * KN + k) * XN + x).astype(F32), 2 * short_count, hot_count)
    g_s[4 * quarter :, :] = pair_grad(scores[4 * quarter :, :], tag, 0.0)

    grads = g_s[...]
    terms = dot(grads, docs_s[...], 1, 0)
    for s, c in enumerate((c0, c1, c2, c3)):
        c[...] = terms[s * quarter : (s + 1) * quarter, :].astype(BF)
    hotp[...] = terms[4 * quarter :, :].astype(BF)
    back = dot(grads, w_s[...], 0, 0)
    mine[...] = back[: 4 * rows, :].astype(BF)
    other[...] = back[4 * rows :, :].astype(BF)


def scores_stage(msgs, quarters, hot_weight, short_count, hot_count, labels):
    rows, width = msgs[0].shape[0] - META, msgs[0].shape[1]
    quarter = quarters[0].shape[0]
    total = 4 * quarter + labels
    flops = 3 * 2 * 8 * rows * total * width
    hbm = pl.BlockSpec(memory_space=pl.ANY)
    vmem = pl.BlockSpec(memory_space=pltpu.VMEM)

    def body(*refs):
        scores_kernel(short_count, hot_count, *refs)

    part = jax.ShapeDtypeStruct((quarter, width), BF)
    return pl.pallas_call(
        body,
        in_specs=[hbm] * 13,
        out_specs=[vmem] * 7,
        out_shape=(
            jax.ShapeDtypeStruct((4 * rows, width), BF),
            jax.ShapeDtypeStruct((4 * rows, width), BF),
            jax.ShapeDtypeStruct((labels, width), BF),
            part,
            part,
            part,
            part,
        ),
        scratch_shapes=[
            pltpu.VMEM((8 * rows, width), BF),
            pltpu.VMEM((8, META, rows), BF),
            pltpu.VMEM((total, width), BF),
            pltpu.VMEM((total, 8 * rows), BF),
            pltpu.SemaphoreType.DMA((21,)),
        ],
        cost_estimate=pl.CostEstimate(
            flops=flops, bytes_accessed=5 << 20, transcendentals=8 * rows * total
        ),
        name="scores",
    )(*msgs, *quarters, hot_weight)


def fast_form(documents, cold_weight, hot_weight, shortlist, positives, hot_ids, hot_labels):
    rows, width = documents.shape
    labels = cold_weight.shape[1]
    _, x, y, k = position()
    msg, quarter = prep(documents, shortlist, positives, hot_ids, hot_labels, cold_weight)
    near = [msg] + [send(msg, p) for p in (TO_X, TO_Y, TO_XY)]
    quarters = [quarter] + [send(quarter, TO_Z[s]) for s in (1, 2, 3)]
    far = [send(m, TO_K) for m in near]
    mine, other, hotp, c0, c1, c2, c3 = scores_stage(
        near + far, quarters, hot_weight, shortlist.shape[1], hot_ids.shape[1], labels
    )
    pair = (hotp.astype(F32) + send(hotp, PAIR_Z1).astype(F32)).astype(BF)
    full = (pair.astype(F32) + send(pair, PAIR_Z2).astype(F32)).astype(BF)
    side = send(full, TO_X)
    grad_hot = jnp.where(
        x == 0, jnp.concatenate([full, side], axis=0), jnp.concatenate([side, full], axis=0)
    ).astype(F32)
    back = [send(c, TO_Z[4 - s]) for s, c in ((1, c1), (2, c2), (3, c3))]
    summed = c0.astype(F32)
    for b in back:
        summed = summed + b.astype(F32)
    summed = summed.astype(BF)
    across = send(summed, TO_Y)
    summed_k, across_k = send(summed, TO_K), send(across, TO_K)

    def ordered(a, b):
        return jnp.where(
            k == 0, jnp.concatenate([a, b], axis=0), jnp.concatenate([b, a], axis=0)
        )

    own_c, other_c = ordered(summed, summed_k), ordered(across, across_k)
    grad_cold = jnp.where(
        y == 0, jnp.stack([own_c, other_c]), jnp.stack([other_c, own_c])
    ).astype(F32)
    both = (mine.astype(F32) + send(other, TO_K).astype(F32)).astype(BF)
    parts = [both[i * rows : (i + 1) * rows] for i in range(4)]
    grad = parts[0].astype(F32)
    for p, pairs in zip(parts[1:], (TO_X, TO_Y, TO_XY)):
        grad = grad + send(p, pairs).astype(F32)
    return grad_cold, grad_hot, grad.astype(BF)


def solution(mesh):
    fast = mesh.shape["cl"] == ZN * XN and mesh.shape["hot"] == YN * KN

    def on_device(*args):
        cold_weight, hot_weight = args[1], args[2]
        same = cold_weight.shape[0] == YN and hot_weight.shape[0] == XN * cold_weight.shape[1]
        return fast_form(*args) if fast and same else general_form(*args)

    return jax.shard_map(
        on_device,
        mesh=mesh,
        in_specs=(
            P(("cl", "hot"), None),
            P("cl", None, None),
            P("hot", None),
            P(("cl", "hot"), None),
            P(("cl", "hot"), None),
            P(("cl", "hot"), None),
            P(("cl", "hot"), None),
        ),
        out_specs=(P("cl", None, None), P("hot", None), P(("cl", "hot"), None)),
        check_vma=False,
    )
```
